32 devices in a mesh: dp: 8 (over z, y), fsdp: 4 (over x, core).
Axes of the slice: x: 2, y: 2, z: 4, core: 2. Of those that a mesh axis runs over, the one named last changes fastest.
Arguments:
- tokens: bfloat16 [64, 128, 1024], P(('dp', 'fsdp')), may hold values from -6 to 6
- cotangent: bfloat16 [64, 128, 1024], P(('dp', 'fsdp')), may hold values from -6 to 6
- lengths: int32 [64], replicated, may hold values from 32 to 128, as said below
- slot_of_block: int32 [4, 192], P('fsdp'), may hold values from 0 to 191, as said below
- master_blocks: float32 [4, 192, 128, 128], P('fsdp', 'dp')
- left_state: float32 [4, 192, 128, 128], P('fsdp', 'dp'), as said below
- right_state: float32 [4, 192, 128, 128], P('fsdp', 'dp'), as said below
- left_root: float32 [4, 192, 128, 128], P('fsdp', 'dp'), as said below
- right_root: float32 [4, 192, 128, 128], P('fsdp', 'dp'), as said below
- vec_master: float32 [13312], replicated
- vec_first: float32 [13312], replicated, may hold values from -0.6 to 0.6
- vec_second: float32 [13312], replicated, may hold values from 0.01 to 0.1
Outputs:
- block_out: bfloat16 [64, 128, 1024], P(('dp', 'fsdp'))
- input_grad: float32 [64, 128, 1024], P(('dp', 'fsdp'))
- grad_blocks: float32 [4, 192, 128, 128], P('fsdp', 'dp')
- new_left: float32 [4, 192, 128, 128], P('fsdp', 'dp')
- new_right: float32 [4, 192, 128, 128], P('fsdp', 'dp')
- new_master: float32 [4, 192, 128, 128], P('fsdp', 'dp')
- vec_grad: float32 [13312], replicated
- new_first: float32 [13312], replicated
- new_second: float32 [13312], replicated
- new_vec: float32 [13312], replicated
The draws below stay inside these ranges and needn't reach their ends.
Inputs may be any that keep to these rules, and one draw needn't show every extreme that they name: `lengths`: positions from a slot's length on are padding; one slot has 128 and one has 32 valid tokens. `slot_of_block`: each row is a permutation of the 192 slots. `left_state`: each block is symmetric. `right_state`: each block is symmetric. `left_root`: each block is symmetric. `right_root`: each block is symmetric.
All inputs are finite; a program needn't handle non-finite values.
Results may differ from the reference program's by a relative error of at most 0.0033.
The reference program's roundings to bfloat16 on the way count: a program that leaves them out, or rounds other values in their place, can miss the bound.
Values may be sent and summed in bfloat16 or wider, within the bound.
No kernel may reach another device: no remote copies, remote signals or barrier semaphores. Data moves between devices by JAX's collectives and lax.ppermute only.
A program may use at most 256 MiB of HBM per device.

```python
import math
import jax
import jax.numpy as jnp
from jax import lax

D = 1024
HEADS = 16
HEAD = 64
FF = 4096
ROT = 16
SEQ = 128
BLK = 128
STEP = 5
FSHARDS = 4
SB = 192
SLOTS = 64
NVEC = 13312
N_FSDP = 4


def owner_order(key):
    row_keys = jax.random.split(jax.random.fold_in(key, 11), FSHARDS)
    return jax.vmap(lambda sub_key: jax.random.permutation(sub_key, SB))(row_keys).astype(jnp.int32)


def draw_slot_of_block(key, part):
    return owner_order(key)


def draw_master_blocks(key, part):
    rows_shard = D // FSHARDS
    count_qkv = rows_shard // BLK * (3 * D // BLK)
    count_out = rows_shard // BLK * (D // BLK)
    count_up = rows_shard // BLK * (FF // BLK)
    block_index = jnp.arange(SB)
    block_scale = jnp.where(block_index < count_qkv, D ** (-0.5), jnp.where(block_index < count_qkv + count_out, max(D // 64, 1) ** (-0.5), jnp.where(block_index < count_qkv + count_out + count_up, D ** (-0.5), FF ** (-0.5)))).astype(jnp.float32)
    slot_order = owner_order(key)
    slot_scale = jax.vmap(lambda row_order: jnp.zeros((SB,), jnp.float32).at[row_order].set(block_scale))(slot_order)
    normals = jax.random.normal(jax.random.fold_in(key, 12), (FSHARDS, SB, BLK, BLK), jnp.float32)
    return normals * slot_scale[:, :, None, None]


def symmetric_draw(key, base):
    normals = jax.random.normal(key, (FSHARDS, SB, BLK, BLK), jnp.float32)
    mixed_part = (normals + jnp.swapaxes(normals, -1, -2)) * (0.03 / 2 ** 0.5)
    return base * (jnp.eye(BLK, dtype=jnp.float32) + mixed_part)


def scaled_symmetric(key, base):
    core = symmetric_draw(jax.random.fold_in(key, 1), base)
    factors = jnp.exp(jax.random.uniform(jax.random.fold_in(key, 2), (FSHARDS, SB, BLK), jnp.float32, 0.0, 1.1))
    return core * factors[..., :, None] * factors[..., None, :]


def draw_left_state(key, part):
    return symmetric_draw(jax.random.fold_in(key, 21), 20.0)


def draw_right_state(key, part):
    return symmetric_draw(jax.random.fold_in(key, 22), 20.0)


def draw_left_root(key, part):
    return scaled_symmetric(jax.random.fold_in(key, 23), 0.5)


def draw_right_root(key, part):
    return scaled_symmetric(jax.random.fold_in(key, 24), 0.5)


def draw_vec_master(key, part):
    index_vec = jnp.arange(NVEC)
    gain_zone = (index_vec < D) | (index_vec >= 2 * D) & (index_vec < 3 * D)
    gains = 1.0 + jax.random.uniform(jax.random.fold_in(key, 31), (NVEC,), jnp.float32, -0.3, 0.3)
    biases = 0.3 * jax.random.normal(jax.random.fold_in(key, 32), (NVEC,), jnp.float32)
    return jnp.where(gain_zone, gains, biases)


def draw_lengths(key, part):
    drawn = jax.random.randint(jax.random.fold_in(key, 41), (SLOTS,), SEQ // 4, SEQ + 1, jnp.int32)
    chosen = jax.random.randint(jax.random.fold_in(key, 42), (), 0, SLOTS, jnp.int32)
    drawn = drawn.at[chosen].set(SEQ)
    return drawn.at[(chosen + 1) % SLOTS].set(SEQ // 4)


def steps_of(stream_key, shape, cuts, smallest, top_value):
    def one(dim, parts):
        steps = jax.random.uniform(jax.random.fold_in(jax.random.fold_in(stream_key, 6), dim), (parts,), jnp.float32, smallest / len(cuts), top_value / len(cuts))
        return jnp.repeat(jnp.exp(steps), shape[dim] // parts).reshape((-1,) + (1,) * (len(shape) - dim - 1))

    loudness = one(*cuts[0])
    for cut in cuts[1:]:
        loudness = loudness * one(*cut)
    return loudness


def scatter_about(stream_key, shape, scale, most, cuts=(), kind=jnp.bfloat16):
    loudness = steps_of(stream_key, shape, cuts, -0.22, 0.18) if cuts else 1.0
    values = jax.random.normal(stream_key, shape, jnp.float32) * scale * loudness
    return jnp.minimum(jnp.maximum(values, -most), most).astype(kind)


def setup_inputs(seed: int = 0) -> dict:
    streams_of = jax.random.split(jax.random.key(seed), 13)
    tokens = scatter_about(streams_of[0], (SLOTS, SEQ, D), 1.0, 6.0, ((0, 32),))
    cotangent = scatter_about(streams_of[1], (SLOTS, SEQ, D), 1.0, 6.0, ((0, 32),))
    lengths = draw_lengths(jax.random.fold_in(streams_of[12], 71), 0)
    slot_of_block = draw_slot_of_block(jax.random.fold_in(streams_of[12], 71), 0)
    master_blocks = draw_master_blocks(jax.random.fold_in(streams_of[12], 71), 0)
    left_state = draw_left_state(jax.random.fold_in(streams_of[12], 71), 0)
    right_state = draw_right_state(jax.random.fold_in(streams_of[12], 71), 0)
    left_root = draw_left_root(jax.random.fold_in(streams_of[12], 71), 0)
    right_root = draw_right_root(jax.random.fold_in(streams_of[12], 71), 0)
    vec_master = draw_vec_master(jax.random.fold_in(streams_of[12], 71), 0)
    vec_first = scatter_about(streams_of[10], (NVEC,), 0.1, 0.6, (), jnp.float32)
    vec_second = jnp.clip(jnp.exp(jax.random.uniform(streams_of[11], (NVEC,), jnp.float32, math.log(0.01), math.log(0.1))), 0.01, 0.1)
    return dict(tokens=tokens, cotangent=cotangent, lengths=lengths, slot_of_block=slot_of_block, master_blocks=master_blocks, left_state=left_state, right_state=right_state, left_root=left_root, right_root=right_root, vec_master=vec_master, vec_first=vec_first, vec_second=vec_second)


@jax.custom_vjp
def low(v):
    return lax.optimization_barrier(v.astype(jnp.bfloat16)).astype(jnp.float32)

@jax.custom_vjp
def low_back(v):
    return v

def low_keep(v):
    return (low(v), None)

def low_pass(kept, grad):
    return (grad,)

def back_keep(v):
    return (v, None)

def back_low(kept, grad):
    return (low(grad),)
low.defvjp(low_keep, low_pass)
low_back.defvjp(back_keep, back_low)

def layer_norm(values, gain_vec, bias_vec):
    centre = lax.optimization_barrier(jnp.mean(values, axis=-1, keepdims=True))
    spread = lax.optimization_barrier(jnp.mean(jnp.square(values - centre), axis=-1, keepdims=True))
    return (values - centre) * lax.rsqrt(spread + 1e-05) * gain_vec + bias_vec

def rotary_tables(length):
    positions = jnp.arange(length).astype(jnp.float32)
    frequency = 10000.0 ** (-jnp.arange(0, ROT, 2).astype(jnp.float32) / ROT)
    angles = positions[:, None] * frequency[None, :]
    angles = jnp.concatenate([angles, angles], axis=-1)[:, None, :]
    return (jnp.cos(angles), jnp.sin(angles))

def apply_rotary(values, cosine_table, sine_table):
    moving = values[..., :ROT]
    first_half = moving[..., :ROT // 2]
    second_half = moving[..., ROT // 2:]
    turned = moving * cosine_table + jnp.concatenate([-second_half, first_half], axis=-1) * sine_table
    return jnp.concatenate([turned, values[..., ROT:]], axis=-1)

def split_vectors(vectors):
    bounds = [D, D, D, D, 3 * D, D, FF, D]
    pieces = []
    offset = 0
    for extent in bounds:
        pieces.append(vectors[offset:offset + extent])
        offset = offset + extent
    return pieces

def shard_shapes(shards):
    return [(D // shards, 3 * D), (D // shards, D), (D // shards, FF), (FF // shards, D)]

def unblock_all(ordered, shapes):
    matrices = []
    offset = 0
    for rows_count, cols_count in shapes:
        number = rows_count // BLK * (cols_count // BLK)
        tile_grid = ordered[offset:offset + number].reshape(rows_count // BLK, cols_count // BLK, BLK, BLK)
        matrices.append(tile_grid.transpose(0, 2, 1, 3).reshape(rows_count, cols_count))
        offset = offset + number
    return matrices

def to_blocks(matrix):
    rows_count, cols_count = matrix.shape
    tile_grid = matrix.reshape(rows_count // BLK, BLK, cols_count // BLK, BLK)
    return tile_grid.transpose(0, 2, 1, 3).reshape(-1, BLK, BLK)

def shampoo_update(grads_in, left_old, right_old, left_inv, right_inv, master, grad_scale):
    highest = lax.Precision.HIGHEST
    scaled = grads_in * grad_scale
    new_left = 0.5 * left_old + 0.5 * jnp.einsum('abij,abkj->abik', scaled, scaled, precision=highest)
    new_right = 0.5 * right_old + 0.5 * jnp.einsum('abji,abjk->abik', scaled, scaled, precision=highest)
    direction = jnp.einsum('abij,abjk->abik', left_inv, scaled, precision=highest)
    direction = jnp.einsum('abij,abjk->abik', direction, right_inv, precision=highest)
    norm_inv = lax.rsqrt(lax.optimization_barrier(jnp.mean(jnp.square(direction), axis=(2, 3), keepdims=True)) + 1e-06)
    return (new_left, new_right, master - 0.03 * direction * norm_inv)

def adam_update(grads_in, first_old, second_old, master, grad_scale):
    scaled = grads_in * grad_scale
    first_new = 0.9 * first_old + 0.1 * scaled
    second_new = 0.95 * second_old + 0.05 * scaled * scaled
    fixed_one = 1.0 - 0.9 ** STEP
    fixed_two = 1.0 - 0.95 ** STEP
    return (first_new, second_new, master - 0.03 * (first_new / fixed_one) / (jnp.sqrt(second_new / fixed_two) + 1e-08))

def forward(params, inputs, lengths_group):
    w_qkv, w_out, w_up, w_down, vectors = params
    gain_one, bias_one, gain_two, bias_two, bias_qkv, bias_out, bias_up, bias_down = split_vectors(vectors)
    w_qkv, w_out, w_up, w_down = (low(w_qkv), low(w_out), low(w_up), low(w_down))
    highest = lax.Precision.HIGHEST
    group_size, length = (inputs.shape[0], inputs.shape[1])
    cosine_table, sine_table = rotary_tables(length)
    normed_one = low(layer_norm(inputs, gain_one, bias_one))
    normed_two = low(layer_norm(inputs, gain_two, bias_two))
    projected = low_back(jnp.einsum('gsd,de->gse', normed_one, w_qkv, precision=highest) + bias_qkv)
    heads_shape = (group_size, length, HEADS, HEAD)
    queries = low(apply_rotary(projected[..., :D].reshape(heads_shape), cosine_table, sine_table))
    keys_all = low(apply_rotary(projected[..., D:2 * D].reshape(heads_shape), cosine_table, sine_table))
    values_all = low(projected[..., 2 * D:].reshape(heads_shape))
    scores = low_back(jnp.einsum('gqhd,gkhd->ghqk', queries, keys_all, precision=highest) * HEAD ** (-0.5))
    positions = jnp.arange(length)
    allowed = (positions[None, None, :] <= positions[None, :, None]) & (positions[None, None, :] < lengths_group[:, None, None])
    scores = jnp.where(allowed[:, None, :, :], scores, -1e+30)
    weights = low(jax.nn.softmax(scores, axis=-1))
    context = low(low_back(jnp.einsum('ghqk,gkhd->gqhd', weights, values_all, precision=highest)))
    context = context.reshape(group_size, length, D)
    attended = jnp.einsum('gsd,de->gse', context, w_out, precision=highest) + bias_out
    pre_act = low_back(jnp.einsum('gsd,df->gsf', normed_two, w_up, precision=highest) + bias_up)
    hidden = low(jax.nn.gelu(pre_act, approximate=False))
    lowered = jnp.einsum('gsf,fd->gsd', hidden, w_down, precision=highest) + bias_down
    return inputs + attended + lowered

def reference(tokens, cotangent, lengths, slot_of_block, master_blocks, left_state, right_state, left_root, right_root, vec_master, vec_first, vec_second):
    shapes = shard_shapes(N_FSDP)
    collected = [[], [], [], []]
    for shard_index in range(N_FSDP):
        ordered = master_blocks[shard_index][slot_of_block[shard_index]]
        for position, matrix in enumerate(unblock_all(ordered, shapes)):
            collected[position].append(matrix)
    weights = [jnp.concatenate(column, axis=0) for column in collected]
    params = (weights[0], weights[1], weights[2], weights[3], vec_master)
    group_size = 8
    rounds = SLOTS // group_size
    token_groups = tokens.reshape(rounds, group_size, SEQ, D)
    seed_groups = cotangent.reshape(rounds, group_size, SEQ, D)
    length_groups = lengths.reshape(rounds, group_size)

    def run_group(totals, group_item):
        inputs, seed_rows, lengths_group = group_item
        inputs32 = inputs.astype(jnp.float32)
        valid_mask = (jnp.arange(SEQ)[None, :] < lengths_group[:, None]).astype(jnp.float32)
        result, pullback = jax.vjp(lambda weights_in, values_in: forward(weights_in, values_in, lengths_group), params, inputs32)
        param_grads, input_grads = pullback(seed_rows.astype(jnp.float32) * valid_mask[:, :, None])
        totals = jax.tree.map(lambda left_val, right_val: left_val + right_val, totals, param_grads)
        return (totals, (result.astype(jnp.bfloat16), input_grads))
    initial = jax.tree.map(jnp.zeros_like, params)
    totals, (outputs, input_grads) = lax.scan(run_group, initial, (token_groups, seed_groups, length_groups))
    rows_shard = [dims_pair[0] for dims_pair in shapes]
    slot_grads = []
    for shard_index in range(N_FSDP):
        tile_lists = [to_blocks(totals[position][shard_index * rows_shard[position]:(shard_index + 1) * rows_shard[position]]) for position in range(4)]
        block_grads = jnp.concatenate(tile_lists, axis=0)
        slot_grads.append(jnp.zeros_like(block_grads).at[slot_of_block[shard_index]].set(block_grads))
    grad_blocks = jnp.stack(slot_grads)
    grad_scale = lax.rsqrt(jnp.sum(lengths).astype(jnp.float32))
    new_left, new_right, new_master = shampoo_update(grad_blocks, left_state, right_state, left_root, right_root, master_blocks, grad_scale)
    vec_grad = totals[4]
    new_first, new_second, new_vec = adam_update(vec_grad, vec_first, vec_second, vec_master, grad_scale)
    return (outputs.reshape(SLOTS, SEQ, D), input_grads.reshape(SLOTS, SEQ, D), grad_blocks, new_left, new_right, new_master, vec_grad, new_first, new_second, new_vec)
```

```python
import jax
import jax.numpy as jnp
import numpy as np
from jax import lax
from jax.experimental import pallas as pl
from jax.experimental.pallas import tpu as pltpu
from jax.sharding import PartitionSpec as P

D = 1024
HEADS = 16
HEAD = 64
FF = 4096
ROT = 16
BLK = 128
STEP = 5
TILE = 256
AXES = ("dp", "fsdp")
F32 = jnp.float32
BF16 = jnp.bfloat16


def dot(left, right):
    return lax.dot_general(left, right, (((1,), (0,)), ((), ())), preferred_element_type=F32)


def dot_rt(left, right):
    return lax.dot_general(left, right, (((1,), (1,)), ((), ())), preferred_element_type=F32)


def dot_lt(left, right):
    return lax.dot_general(left, right, (((0,), (0,)), ((), ())), preferred_element_type=F32)


def split_vectors(vectors):
    bounds = [D, D, D, D, 3 * D, D, FF, D]
    pieces = []
    offset = 0
    for extent in bounds:
        pieces.append(vectors[offset : offset + extent])
        offset = offset + extent
    return pieces


def adam_update(grads_in, first_old, second_old, master, grad_scale):
    scaled = grads_in * grad_scale
    first_new = 0.9 * first_old + 0.1 * scaled
    second_new = 0.95 * second_old + 0.05 * scaled * scaled
    fixed_one = 1.0 - 0.9**STEP
    fixed_two = 1.0 - 0.95**STEP
    return (
        first_new,
        second_new,
        master - 0.03 * (first_new / fixed_one) / (jnp.sqrt(second_new / fixed_two) + 1e-08),
    )


def shampoo_update(grads_in, left_old, right_old, left_inv, right_inv, master, grad_scale):
    highest = lax.Precision.HIGHEST
    scaled = grads_in * grad_scale
    new_left = 0.5 * left_old + 0.5 * jnp.einsum(
        "abij,abkj->abik", scaled, scaled, precision=highest
    )
    new_right = 0.5 * right_old + 0.5 * jnp.einsum(
        "abji,abjk->abik", scaled, scaled, precision=highest
    )
    direction = jnp.einsum("abij,abjk->abik", left_inv, scaled, precision=highest)
    direction = jnp.einsum("abij,abjk->abik", direction, right_inv, precision=highest)
    norm_inv = lax.rsqrt(jnp.mean(jnp.square(direction), axis=(2, 3), keepdims=True) + 1e-06)
    return (new_left, new_right, master - 0.03 * direction * norm_inv)


def tile_codes(me):
    block = np.arange(192)
    part = np.select([block < 48, block < 64, block < 128], [0, 1, 2], 3)
    local = block - np.array([0, 48, 64, 128])[part]
    wide = np.array([24, 8, 32, 8])[part]
    row, col = local // wide, local % wide
    shard = np.where(part == 0, col % 8 // 2, col // 8)
    fixed = np.select(
        [part == 0, part == 1, part == 2],
        [col // 8, 28 + col // 2, 12 + col % 8 // 2],
        32 + row // 2 * 4 + col // 2,
    )
    stride = np.select([part == 0, part == 2], [3, 4], 0)
    quarter = row % 2 * 2 + col % 2
    relative = jnp.bitwise_xor(jnp.asarray(shard, jnp.int32), me)
    tile = jnp.asarray(fixed, jnp.int32) + jnp.asarray(stride, jnp.int32) * relative
    return tile * 4 + jnp.asarray(quarter, jnp.int32)


def sort_kernel(count, codes, starts, *refs):
    pieces, out, sem = refs[:-2], refs[-2], refs[-1]
    for index, piece in enumerate(pieces):
        start = starts[index]

        def step(item, carry, piece=piece, start=start):
            code = codes[start + item]
            row = pl.multiple_of((code & 2) * 64, BLK)
            col = pl.multiple_of((code & 1) * 128, BLK)
            pltpu.make_async_copy(
                piece.at[item], out.at[code >> 2, pl.ds(row, BLK), pl.ds(col, BLK)], sem
            ).start()
            return carry

        lax.fori_loop(0, count, step, 0, unroll=True)
    pltpu.make_async_copy(out, out, sem).wait()


def sort_blocks(codes, starts, pieces):
    count = pieces[0].shape[0]
    total = count * len(pieces)
    return pl.pallas_call(
        lambda *refs: sort_kernel(count, *refs),
        out_shape=jax.ShapeDtypeStruct((total // 4, TILE, TILE), BF16),
        in_specs=[pl.BlockSpec(memory_space=pltpu.SMEM)] * 2
        + [pl.BlockSpec(memory_space=pl.ANY)] * len(pieces),
        out_specs=pl.BlockSpec(memory_space=pltpu.VMEM),
        scratch_shapes=[pltpu.SemaphoreType.DMA],
        name="sort_blocks",
    )(codes, starts, *pieces)


def scatter_kernel(me_ref, place, *refs):
    ups, qkvs, down, outw, out, sem = refs[0:4], refs[4:8], refs[8], refs[9], refs[10], refs[11]
    me = me_ref[0]

    def send(source, tile, block, row, col):
        pltpu.make_async_copy(
            source.at[tile, pl.ds(row * BLK, BLK), pl.ds(col * BLK, BLK)],
            out.at[place[block]],
            sem,
        ).start()

    for row in range(2):
        for col in range(2):
            for tile in range(16):
                send(down, tile, 128 + (tile // 4 * 2 + row) * 8 + tile % 4 * 2 + col, row, col)
            for tile in range(4):
                send(outw, tile, 48 + row * 8 + tile * 2 + col, row, col)
            for relative in range(4):
                shard = jnp.bitwise_xor(me, relative)
                for tile in range(4):
                    send(ups[relative], tile, 64 + row * 32 + shard * 8 + tile * 2 + col, row, col)
                for tile in range(3):
                    send(qkvs[relative], tile, row * 24 + tile * 8 + shard * 2 + col, row, col)
    pltpu.make_async_copy(out, out, sem).wait()


def scatter_blocks(me, place, ups, qkvs, down, outw):
    return pl.pallas_call(
        scatter_kernel,
        out_shape=jax.ShapeDtypeStruct((place.shape[0], BLK, BLK), BF16),
        in_specs=[pl.BlockSpec(memory_space=pltpu.SMEM)] * 2
        + [pl.BlockSpec(memory_space=pl.ANY)] * 10,
        out_specs=pl.BlockSpec(memory_space=pltpu.VMEM),
        scratch_shapes=[pltpu.SemaphoreType.DMA],
        name="scatter_blocks",
    )(me, place, *ups, *qkvs, down, outw)


def window(shape, index):
    return pl.BlockSpec(shape, lambda i, index=index: index, pipeline_mode=pl.Buffered(1))


def whole(shape):
    return window(shape, (0,) * len(shape))


SMEM = pl.BlockSpec(memory_space=pltpu.SMEM)


def mlp_kernel(
    me_ref, x2, x2t, og, up0, up1, up2, up3, down, bias,
    hidden, pre_grad, d0, d1, d2, d3, d_down, w_up, w_down, sums,
):
    me = me_ref[0]
    rows = x2.shape[0]
    ups, grads = (up0, up1, up2, up3), (d0, d1, d2, d3)
    places = [pl.multiple_of(jnp.bitwise_xor(me, r) * TILE, TILE) for r in range(4)]
    for c in range(4):
        lanes = slice(c * TILE, (c + 1) * TILE)
        for r in range(4):
            w_up[c, pl.ds(places[r], TILE), :] = ups[r][c]
        for n in range(4):
            w_down[lanes, n * TILE : (n + 1) * TILE] = down[c * 4 + n]

        def step(block, total, c=c, lanes=lanes):
            here = pl.ds(pl.multiple_of(block * TILE, TILE), TILE)
            pre = dot(x2[here, :], w_up[c]) + bias[c : c + 1, :]
            upper = dot_rt(og[here, :], w_down[lanes, :])
            cdf = 0.5 * (1.0 + lax.erf(pre * 0.7071067811865476))
            pdf = jnp.exp(-0.5 * pre * pre) * 0.3989422804014327
            hidden[here, lanes] = (pre * cdf).astype(BF16)
            grad = (upper * (cdf + pre * pdf)).astype(BF16)
            pre_grad[here, lanes] = grad
            return total + jnp.sum(grad.astype(F32), axis=0, keepdims=True)

        sums[c : c + 1, :] = lax.fori_loop(
            0, rows // TILE, step, jnp.zeros((1, TILE), F32), unroll=True
        )
        for r in range(4):
            grads[r][c] = dot(x2t[pl.ds(places[r], TILE), :], pre_grad[:, lanes]).astype(BF16)
        hidden_t = hidden[:, lanes].T
        for n in range(4):
            d_down[c * 4 + n] = dot(hidden_t, og[:, n * TILE : (n + 1) * TILE]).astype(BF16)


def mlp_call(me, x2, x2t, og, tiles, ups, bias):
    rows = x2.shape[0]
    tile4 = jax.ShapeDtypeStruct((4, TILE, TILE), BF16)
    outs = [
        jax.ShapeDtypeStruct((rows, D), BF16),
        jax.ShapeDtypeStruct((rows, D), BF16),
        tile4, tile4, tile4, tile4,
        jax.ShapeDtypeStruct((16, TILE, TILE), BF16),
        jax.ShapeDtypeStruct((4, D, TILE), BF16),
        jax.ShapeDtypeStruct((D, D), BF16),
        jax.ShapeDtypeStruct((4, TILE), F32),
    ]
    return pl.pallas_call(
        mlp_kernel,
        grid=(1,),
        out_shape=outs,
        in_specs=[SMEM, whole(x2.shape), whole(x2t.shape), whole(og.shape),
                  window((4, TILE, TILE), (3, 0, 0))]
        + [whole((4, TILE, TILE))] * 3
        + [window((16, TILE, TILE), (2, 0, 0)), whole(bias.shape)],
        out_specs=[whole(o.shape) for o in outs],
        compiler_params=pltpu.CompilerParams(vmem_limit_bytes=60 << 20),
        cost_estimate=pl.CostEstimate(
            flops=8 * rows * D * D, transcendentals=2 * rows * D, bytes_accessed=24 << 20
        ),
        name="mlp",
    )(me, x2, x2t, og, tiles, *ups, tiles, bias)


def attention_kernel(
    me_ref, lens, x1, x1t, og, q0, q1, q2, q3, outw, bias, cosine, sine_a, sine_b,
    context, pg, d0, d1, d2, d3, d_out, w_qkv, w_out, sums,
):
    me = me_ref[0]
    rows = x1.shape[0]
    seq = cosine.shape[0]
    qkvs, grads = (q0, q1, q2, q3), (d0, d1, d2, d3)
    places = [pl.multiple_of(jnp.bitwise_xor(me, r) * TILE, TILE) for r in range(4)]
    heads = TILE // HEAD
    for r in range(4):
        for part in range(3):
            w_qkv[part, pl.ds(places[r], TILE), :] = qkvs[r][part]
    for n in range(4):
        w_out[:, n * TILE : (n + 1) * TILE] = outw[n]
    lane_head = lax.broadcasted_iota(jnp.int32, (seq, TILE), 1) // HEAD
    query = lax.broadcasted_iota(jnp.int32, (seq, seq), 0)
    key = lax.broadcasted_iota(jnp.int32, (seq, seq), 1)
    scale = HEAD ** (-0.5)

    def rotate(values, sign):
        after = jnp.concatenate(
            [pltpu.roll(values[:, :BLK], BLK - ROT // 2, 1), pltpu.roll(values[:, BLK:], BLK - ROT // 2, 1)], axis=1
        )
        before = jnp.concatenate(
            [pltpu.roll(values[:, :BLK], ROT // 2, 1), pltpu.roll(values[:, BLK:], ROT // 2, 1)], axis=1
        )
        turned = after * sine_a[...] + before * sine_b[...]
        return values * cosine[...] + (turned if sign > 0 else -turned)

    def stacked(values):
        return jnp.concatenate(
            [jnp.where(lane_head == h, values, 0.0).astype(BF16) for h in range(heads)], axis=0
        )

    def picked(values):
        total = jnp.where(lane_head == 0, values[:seq], 0.0)
        for h in range(1, heads):
            total = jnp.where(lane_head == h, values[h * seq : (h + 1) * seq], total)
        return total

    def step(block, totals):
        here = pl.ds(pl.multiple_of(block * 2 * seq, 2 * seq), 2 * seq)
        xr = x1[here, :]
        projected = [dot(xr, w_qkv[p]) + bias[p : p + 1, :] for p in range(3)]
        context_grad = dot_rt(og[here, :], w_out[...])
        for sub in range(2):
            now = pl.ds(pl.multiple_of(block * 2 * seq + sub * seq, seq), seq)
            part = slice(sub * seq, (sub + 1) * seq)
            queries = rotate(projected[0][part], 1).astype(BF16).astype(F32)
            keys = rotate(projected[1][part], 1).astype(BF16)
            values = projected[2][part].astype(BF16)
            queries = stacked(queries)
            allowed = (key <= query) & (key < lens[block * 2 + sub])
            allowed = jnp.concatenate([allowed] * heads, axis=0)
            scores = jnp.where(allowed, dot_rt(queries, keys) * scale, -1e30)
            exponent = jnp.exp(scores - jnp.max(scores, axis=-1, keepdims=True))
            probs = exponent / jnp.sum(exponent, axis=-1, keepdims=True)
            probs_b = probs.astype(BF16)
            context[now, :] = picked(dot(probs_b, values)).astype(BF16)
            upper = stacked(context_grad[part].astype(BF16).astype(F32))
            prob_grad = dot_rt(upper, values)
            inner = jnp.sum(probs * prob_grad, axis=-1, keepdims=True)
            score_grad = (probs * (prob_grad - inner)).astype(BF16)
            value_grad = dot_lt(probs_b, upper)
            query_grad = rotate(picked(dot(score_grad, keys)) * scale, -1)
            key_grad = rotate(dot_lt(score_grad, queries) * scale, -1)
            found = []
            for p, grad in enumerate((query_grad, key_grad, value_grad)):
                grad = grad.astype(BF16)
                pg[p, now, :] = grad
                found.append(totals[p] + jnp.sum(grad.astype(F32), axis=0, keepdims=True))
            totals = tuple(found)
        return totals

    zero = jnp.zeros((1, TILE), F32)
    totals = lax.fori_loop(0, rows // (2 * seq), step, (zero, zero, zero))
    for p in range(3):
        sums[p : p + 1, :] = totals[p]
        for r in range(4):
            grads[r][p] = dot(x1t[pl.ds(places[r], TILE), :], pg[p]).astype(BF16)
    context_t = context[...].T
    for n in range(4):
        d_out[n] = dot(context_t, og[:, n * TILE : (n + 1) * TILE]).astype(BF16)


def attention_call(me, lens, x1, x1t, og, tiles, qkvs, bias, tables):
    rows = x1.shape[0]
    tile3 = jax.ShapeDtypeStruct((3, TILE, TILE), BF16)
    outs = [
        jax.ShapeDtypeStruct((rows, TILE), BF16),
        jax.ShapeDtypeStruct((3, rows, TILE), BF16),
        tile3, tile3, tile3, tile3,
        jax.ShapeDtypeStruct((4, TILE, TILE), BF16),
        jax.ShapeDtypeStruct((3, D, TILE), BF16),
        jax.ShapeDtypeStruct((TILE, D), BF16),
        jax.ShapeDtypeStruct((3, TILE), F32),
    ]
    return pl.pallas_call(
        attention_kernel,
        grid=(1,),
        out_shape=outs,
        in_specs=[SMEM, SMEM, whole(x1.shape), whole(x1t.shape), whole(og.shape),
                  window((3, TILE, TILE), (0, 0, 0))]
        + [whole((3, TILE, TILE))] * 3
        + [window((4, TILE, TILE), (7, 0, 0)), whole(bias.shape)]
        + [whole(t.shape) for t in tables],
        out_specs=[whole(o.shape) for o in outs],
        compiler_params=pltpu.CompilerParams(vmem_limit_bytes=60 << 20),
        cost_estimate=pl.CostEstimate(
            flops=6 * rows * D * D, transcendentals=rows * 512, bytes_accessed=14 << 20
        ),
        name="attention",
    )(me, lens, x1, x1t, og, tiles, *qkvs, tiles, bias, *tables)


def post_kernel(
    context, hidden, pg, pre_grad, w_qkv, w_out, w_up, w_down, xhat, gains,
    out_even, out_odd, grad_even, grad_odd, sums,
):
    rows = xhat.shape[0] // 4
    acc = [jnp.zeros((1, D), F32) for _ in range(4)]
    for r in range(4):
        here = slice(r * rows, (r + 1) * rows)
        partial = dot(context[here, :], w_out[...]) + dot(hidden[here, :], w_down[...])
        (out_odd if r % 2 else out_even)[r // 2] = partial
        first = sum(dot_rt(pg[p, here, :], w_qkv[p]) for p in range(3))
        second = sum(
            dot_rt(pre_grad[here, c * TILE : (c + 1) * TILE], w_up[c]) for c in range(4)
        )
        hat = xhat[here, :]
        for index, grad in ((0, first), (2, second)):
            acc[index] = acc[index] + jnp.sum(grad * hat, axis=0, keepdims=True)
            acc[index + 1] = acc[index + 1] + jnp.sum(grad, axis=0, keepdims=True)
        (grad_odd if r % 2 else grad_even)[r // 2] = first * gains[0:1, :] + second * gains[1:2, :]
    for index in range(4):
        sums[index : index + 1, :] = acc[index]


def post_call(context, hidden, pg, pre_grad, w_qkv, w_out, w_up, w_down, xhat, gains):
    rows = xhat.shape[0]
    half = jax.ShapeDtypeStruct((2, rows // 4, D), F32)
    outs = [half, half, half, half, jax.ShapeDtypeStruct((4, D), F32)]
    args = (context, hidden, pg, pre_grad, w_qkv, w_out, w_up, w_down, xhat, gains)
    return pl.pallas_call(
        post_kernel,
        grid=(1,),
        out_shape=outs,
        in_specs=[whole(a.shape) for a in args],
        out_specs=[whole(o.shape) for o in outs],
        compiler_params=pltpu.CompilerParams(vmem_limit_bytes=60 << 20),
        cost_estimate=pl.CostEstimate(
            flops=6 * rows * D * D, transcendentals=0, bytes_accessed=32 << 20
        ),
        name="post",
    )(*args)


def rotary_tables(length):
    positions = jnp.arange(length).astype(F32)
    frequency = 10000.0 ** (-jnp.arange(0, ROT, 2).astype(F32) / ROT)
    angles = positions[:, None] * frequency[None, :]
    cosine, sine = jnp.cos(angles), jnp.sin(angles)
    zero, one = jnp.zeros_like(sine), jnp.ones((length, HEAD - ROT), F32)
    rest = jnp.zeros((length, HEAD - ROT), F32)
    count = TILE // HEAD
    return (
        jnp.tile(jnp.concatenate([cosine, cosine, one], axis=1), (1, count)),
        jnp.tile(jnp.concatenate([-sine, zero, rest], axis=1), (1, count)),
        jnp.tile(jnp.concatenate([zero, sine, rest], axis=1), (1, count)),
    )


def body(
    tokens, cotangent, lengths, slot_of_block, master_blocks, left_state, right_state,
    left_root, right_root, vec_master, vec_first, vec_second,
):
    shards = lax.axis_size("fsdp")
    owners = lax.axis_size("dp")
    groups = owners // 2
    share = master_blocks.shape[1]
    micro, length = tokens.shape[0], tokens.shape[1]
    own_rows = micro * length
    dp_id, me = lax.axis_index("dp"), lax.axis_index("fsdp")
    group, side = dp_id // 2, dp_id % 2

    def swap_shard(value, mask):
        pairs = [(d * shards + s, d * shards + (s ^ mask)) for d in range(owners) for s in range(shards)]
        return lax.ppermute(value, AXES, pairs)

    def swap_owner(value, mask):
        pairs = [(d * shards + s, (d ^ mask) * shards + s) for d in range(owners) for s in range(shards)]
        return lax.ppermute(value, AXES, pairs)

    def shift_group(value, shift):
        pairs = [
            (d * shards + s, ((d // 2 + shift) % groups * 2 + d % 2) * shards + s)
            for d in range(owners)
            for s in range(shards)
        ]
        return lax.ppermute(value, AXES, pairs)

    column = master_blocks[0].astype(BF16)
    same, other, home = [], [], []
    for step in range(groups):
        same.append(column)
        other.append(swap_owner(column, 1))
        home.append((group - step) % groups * 2)
        if step < groups - 1:
            column = shift_group(column, 1)
    home = jnp.stack(home)
    starts = jnp.concatenate([home + side, home + (1 - side)]).astype(jnp.int32) * share
    slot_order = slot_of_block[0]
    codes = jnp.zeros(slot_order.shape, jnp.int32).at[slot_order].set(tile_codes(me))
    tiles = sort_blocks(codes, starts, same + other)

    def collect(value):
        value = value.reshape(own_rows, D)
        across = swap_shard(value, 2)
        return jnp.concatenate([value, swap_shard(value, 1), across, swap_shard(across, 1)], axis=0)

    near = jnp.arange(shards, dtype=jnp.int32) ^ me
    slot_ids = ((dp_id * shards + near)[:, None] * micro + jnp.arange(micro)[None, :]).reshape(-1)
    lens = lengths[slot_ids]
    vectors = split_vectors(vec_master)
    gain_one, bias_one, gain_two, bias_two, bias_qkv, bias_out, bias_up, bias_down = vectors
    inputs = collect(tokens)
    seeds = collect(cotangent)
    valid = (jnp.arange(length)[None, :] < lens[:, None]).reshape(-1, 1)
    out_grad = jnp.where(valid, seeds, jnp.zeros((), BF16))
    values = inputs.astype(F32)
    centre = jnp.mean(values, axis=-1, keepdims=True)
    spread = jnp.mean(jnp.square(values - centre), axis=-1, keepdims=True)
    root = lax.rsqrt(spread + 1e-05)
    xhat = (values - centre) * root
    normed_one = (xhat * gain_one + bias_one).astype(BF16)
    normed_two = (xhat * gain_two + bias_two).astype(BF16)
    me_vec = me.astype(jnp.int32).reshape(1)
    tables = rotary_tables(length)
    my_bias_qkv = lax.dynamic_index_in_dim(bias_qkv.reshape(3, shards, TILE), me, 1, keepdims=False)
    my_bias_up = lax.dynamic_index_in_dim(bias_up.reshape(shards, 4, TILE), me, 0, keepdims=False)

    ups = [swap_shard(tiles[12 + 4 * r : 16 + 4 * r], r) for r in range(1, 4)]
    qkvs = [swap_shard(tiles[3 * r : 3 * r + 3], r) for r in range(1, 4)]
    (hidden, pre_grad, u0, u1, u2, u3, d_down, w_up, w_down, up_sums) = mlp_call(
        me_vec, normed_two, normed_two.T, out_grad, tiles, ups, my_bias_up
    )
    up_grads = [u0] + [swap_shard(u, r) for r, u in ((1, u1), (2, u2), (3, u3))]
    (context, pg, g0, g1, g2, g3, d_out, w_qkv, w_out, qkv_sums) = attention_call(
        me_vec, lens, normed_one, normed_one.T, out_grad, tiles, qkvs, my_bias_qkv, tables
    )
    qkv_grads = [g0] + [swap_shard(g, r) for r, g in ((1, g1), (2, g2), (3, g3))]

    slot_owner, slot_item = slot_order // share, slot_order % share
    place = (
        jnp.bitwise_xor(slot_owner % 2, side) * groups + (slot_owner // 2 - group) % groups
    ) * share + slot_item
    stored = scatter_blocks(me_vec, place.astype(jnp.int32), up_grads, qkv_grads, d_down, d_out)
    owned = None
    order = sorted(range(1, groups), key=lambda s: -min(s, groups - s)) + [0]
    arrived = []
    for shift in order:
        mine = stored[shift * share : (shift + 1) * share]
        theirs = swap_owner(stored[(groups + shift) * share : (groups + shift + 1) * share], 1)
        both = mine.astype(F32) + theirs.astype(F32)
        if shift:
            arrived.append(shift_group(both.astype(BF16), shift))
        else:
            owned = both
    for value in arrived:
        owned = owned + value.astype(F32)
    owned = owned[None]

    gains = jnp.stack([gain_one, gain_two])
    out_even, out_odd, grad_even, grad_odd, norm_sums = post_call(
        context, hidden, pg, pre_grad, w_qkv, w_out, w_up, w_down, xhat, gains
    )

    def reduce_rows(even, odd):
        both = even + swap_shard(odd, 1)
        return both[0] + swap_shard(both[1], 2)

    out_sum = reduce_rows(out_even, out_odd)
    own_x = values[:own_rows]
    block_out = (own_x + out_sum + (bias_out + bias_down)).astype(BF16)
    grad_sum = reduce_rows(grad_even, grad_odd)
    own_hat = xhat[:own_rows]
    own_grad = out_grad[:own_rows].astype(F32)
    input_grad = own_grad + root[:own_rows] * (
        grad_sum
        - jnp.mean(grad_sum, axis=-1, keepdims=True)
        - own_hat * jnp.mean(grad_sum * own_hat, axis=-1, keepdims=True)
    )
    seed_sum = jnp.sum(own_grad, axis=0)
    all_qkv = lax.dynamic_update_index_in_dim(
        jnp.zeros((3, shards, TILE), F32), qkv_sums, me, 1
    )
    all_up = lax.dynamic_update_index_in_dim(jnp.zeros((shards, 4, TILE), F32), up_sums, me, 0)
    vec_grad = jnp.concatenate(
        [norm_sums.reshape(-1), all_qkv.reshape(-1), seed_sum, all_up.reshape(-1), seed_sum]
    ).reshape(-1, BLK)
    for mask in (1, 2):
        vec_grad = vec_grad + swap_shard(vec_grad, mask)
    mask = 1
    while mask < owners:
        vec_grad = vec_grad + swap_owner(vec_grad, mask)
        mask *= 2
    vec_grad = vec_grad.reshape(-1)

    grad_scale = lax.rsqrt(jnp.sum(lengths).astype(F32))
    new_left, new_right, new_master = shampoo_update(
        owned, left_state, right_state, left_root, right_root, master_blocks, grad_scale
    )
    new_first, new_second, new_vec = adam_update(
        vec_grad, vec_first, vec_second, vec_master, grad_scale
    )
    return (
        block_out.reshape(tokens.shape),
        input_grad.reshape(tokens.shape),
        owned, new_left, new_right, new_master,
        vec_grad, new_first, new_second, new_vec,
    )


def solution(mesh):
    rows = P(("dp", "fsdp"), None, None)
    blocks = P("fsdp", "dp", None, None)
    placed = (
        rows, rows, P(), P("fsdp", None),
        blocks, blocks, blocks, blocks, blocks,
        P(), P(), P(),
    )
    return jax.shard_map(
        body,
        mesh=mesh,
        in_specs=placed,
        out_specs=(rows, rows, blocks, blocks, blocks, blocks, P(), P(), P(), P()),
        check_vma=False,
    )
```
